512 devices in a mesh: layer: 8 (over x, core), example: 64 (over z, y).
Axes of the slice: x: 4, y: 4, z: 16, core: 2. Of those that a mesh axis runs over, the one named last changes fastest.
Arguments:
- adapter_input: bfloat16 [8, 8, 262144], P('layer', None, 'example'), may hold values from -4 to 4
- output_gradient: bfloat16 [8, 262144, 512], P('layer', 'example'), may hold values from -4 to 4
- projection: bfloat16 [8, 4, 512, 128], P('layer'), may hold values from -0.25 to 0.25
- input_block_index: int32 [8, 4, 4], P('layer'), may hold values from 0 to 31
- turn_token_length: int32 [8192], P('example'), may hold values from 1 to 32, as said below
- turn_to_example: int32 [8192], P('example'), may hold values from 0 to 4095, as said below
Outputs:
- factor: float32 [512, 512], P('example')
- whitened: float32 [4096, 512], P(('example', 'layer'))
The draws below stay inside these ranges and needn't reach their ends.
Inputs may be any that keep to these rules, and one draw needn't show every extreme that they name: `turn_token_length`: within each shard of 128 turns the lengths add up to at most 4096. `turn_to_example`: the turns of shard s carry the example numbers s * 64 to (s + 1) * 64 - 1, never falling, each at least once.
All inputs are finite; a program needn't handle non-finite values.
Results may differ from the reference program's by a relative error of at most 0.0033.
Values sent between devices are 32-bit elements; how exact they have to be, the bound alone decides.
No kernel may reach another device: no remote copies, remote signals or barrier semaphores. Data moves between devices by JAX's collectives and lax.ppermute only.
A program may use at most 64 MiB of HBM per device.

```python
import math
import jax
import jax.numpy as jnp
from jax import lax

KV = 512
ADAPTER_RANK = 8
F = 512
NPICK = 4
MAXLEN = 32
EX_DEV = 64
TURNS_DEV = 128
SHARD_TOKENS = 4096
FBLK = 4
NBLK = 32
LAYER_COUNT = 8
TURNS = 8192
TOKEN_SLOTS = 262144
EXAMPLES = 4096


def draw_turn_token_length(key, part):
    shards = TURNS // TURNS_DEV
    key_caps, key_busy, key_raw, key_long = jax.random.split(jax.random.fold_in(key, 11), 4)
    caps = jax.random.randint(key_caps, (shards,), 1, MAXLEN + 1)
    busiest = jax.random.randint(key_busy, (), 0, shards)
    shard_ids = jnp.arange(shards)
    caps = jnp.where(shard_ids == busiest, MAXLEN, caps)
    raw_bits = jax.random.randint(key_raw, (shards, TURNS_DEV), 0, 1 << 20)
    lengths = 1 + raw_bits % caps[:, None]
    longest = jax.random.randint(key_long, (), 0, TURNS_DEV)
    chosen = (shard_ids[:, None] == busiest) & (jnp.arange(TURNS_DEV)[None, :] == longest)
    lengths = jnp.where(chosen, MAXLEN, lengths)
    return lengths.reshape(-1).astype(jnp.int32)


def draw_turn_to_example(key, part):
    shards = TURNS // TURNS_DEV
    shard_keys = jax.random.split(jax.random.fold_in(key, 23), shards)

    def one_shard(shard_key):
        order = jax.random.permutation(shard_key, TURNS_DEV - 1)
        cuts = (order < EX_DEV - 1).astype(jnp.int32)
        return jnp.concatenate([jnp.zeros((1,), jnp.int32), jnp.cumsum(cuts).astype(jnp.int32)])
    local_ids = jax.vmap(one_shard)(shard_keys)
    offsets = EX_DEV * jnp.arange(shards, dtype=jnp.int32)
    return (local_ids + offsets[:, None]).reshape(-1).astype(jnp.int32)


def touch_ends(values, stream_key, low, largest):
    shape = values.shape
    index_at = [jax.random.randint(jax.random.fold_in(stream_key, axis), (), 0, shape[axis]) for axis in range(len(shape))]
    values = values.at[tuple(index_at)].set(low)
    longest = shape.index(max(shape))
    index_at[longest] = (index_at[longest] + 1) % shape[longest]
    return values.at[tuple(index_at)].set(largest)


def block_scale(key, dims, cuts, smallest, largest):
    def one(dim, parts):
        heights = jax.random.uniform(jax.random.fold_in(jax.random.fold_in(key, 6), dim), (parts,), jnp.float32, smallest / len(cuts), largest / len(cuts))
        return jnp.repeat(jnp.exp(heights), dims[dim] // parts).reshape((-1,) + (1,) * (len(dims) - dim - 1))

    loudness = one(*cuts[0])
    for cut in cuts[1:]:
        loudness = loudness * one(*cut)
    return loudness


def bell_draw(own_key, dims, width, limit, cuts=(), held_as=jnp.bfloat16):
    loudness = block_scale(own_key, dims, cuts, -0.22, 0.18) if cuts else 1.0
    drawn = jax.random.normal(own_key, dims, jnp.float32) * width * loudness
    return jnp.minimum(jnp.maximum(drawn, -limit), limit).astype(held_as)


def setup_inputs(seed: int = 0) -> dict:
    key_list = jax.random.split(jax.random.key(seed), 7)
    adapter_input = bell_draw(key_list[0], (LAYER_COUNT, ADAPTER_RANK, TOKEN_SLOTS), 0.5, 4.0, ((0, 8), (2, 64)))
    output_gradient = bell_draw(key_list[1], (LAYER_COUNT, TOKEN_SLOTS, KV), 0.5, 4.0, ((0, 8), (1, 64)))
    projection = bell_draw(key_list[2], (LAYER_COUNT, FBLK, NPICK * 128, 128), (NPICK * 128) ** -0.5, 0.25, ((0, 8),))
    input_block_index = touch_ends(jax.random.randint(key_list[3], (LAYER_COUNT, FBLK, NPICK), 0, NBLK), jax.random.fold_in(key_list[3], 1), 0, NBLK - 1).astype(jnp.int32)
    turn_token_length = draw_turn_token_length(jax.random.fold_in(key_list[6], 71), 0)
    turn_to_example = draw_turn_to_example(jax.random.fold_in(key_list[6], 71), 0)
    return dict(adapter_input=adapter_input, output_gradient=output_gradient, projection=projection, input_block_index=input_block_index, turn_token_length=turn_token_length, turn_to_example=turn_to_example)


def slot_owners(turn_token_length, turn_to_example):
    shards = TURNS // TURNS_DEV
    lengths = turn_token_length.reshape(shards, TURNS_DEV).astype(jnp.int32)
    offsets = (EX_DEV * jnp.arange(shards, dtype=jnp.int32))[:, None]
    owners = turn_to_example.reshape(shards, TURNS_DEV).astype(jnp.int32) - offsets
    turn_ends = jnp.cumsum(lengths, axis=1).astype(jnp.int32)
    starts = turn_ends - lengths
    position = jnp.arange(SHARD_TOKENS, dtype=jnp.int32)
    inside = (position[None, None, :] >= starts[:, :, None]) & (position[None, None, :] < turn_ends[:, :, None])
    marked = lax.optimization_barrier(jnp.sum(jnp.where(inside, owners[:, :, None] + 1, 0), axis=1)).astype(jnp.int32) - 1
    return jnp.where(marked < 0, EX_DEV, marked).astype(jnp.int32)

def reference(adapter_input, output_gradient, projection, input_block_index, turn_token_length, turn_to_example):
    shards = TURNS // TURNS_DEV
    owner_all = slot_owners(turn_token_length, turn_to_example)

    def shard_features(shard):
        first_token = shard * SHARD_TOKENS
        owner = lax.dynamic_index_in_dim(owner_all, shard, 0, keepdims=False)
        running = jnp.zeros((EX_DEV, F), jnp.float32)
        for layer_number in range(LAYER_COUNT):
            activation_block = lax.dynamic_slice_in_dim(adapter_input[layer_number], first_token, SHARD_TOKENS, 1).astype(jnp.float32)
            grad_block = lax.dynamic_slice_in_dim(output_gradient[layer_number], first_token, SHARD_TOKENS, 0).astype(jnp.float32)
            outer = (activation_block.T[:, :, None] * grad_block[:, None, :]).reshape(SHARD_TOKENS, ADAPTER_RANK * KV)
            gradient_value = jax.ops.segment_sum(outer, owner, num_segments=EX_DEV + 1)[:EX_DEV].astype(jnp.bfloat16)
            blocks = gradient_value.reshape(EX_DEV, NBLK, 128)
            pieces = []
            for column in range(FBLK):
                chosen = jnp.take(blocks, input_block_index[layer_number, column], axis=1).reshape(EX_DEV, NPICK * 128)
                pieces.append(jnp.dot(chosen.astype(jnp.float32), projection[layer_number, column].astype(jnp.float32), preferred_element_type=jnp.float32))
            running = running + jnp.concatenate(pieces, axis=1)
        return running
    features = lax.map(shard_features, jnp.arange(shards, dtype=jnp.int32)).reshape(EXAMPLES, F)
    gram = jnp.dot(features.T.astype(jnp.float32), features.astype(jnp.float32), precision=lax.Precision.HIGHEST, preferred_element_type=jnp.float32)
    lower_factor = jnp.linalg.cholesky(gram)
    scale = math.sqrt(EXAMPLES)
    factor = lower_factor.T / scale
    whitened = jax.scipy.linalg.solve_triangular(lower_factor, features.T, lower=True).T * scale
    return (factor, whitened)
```

```python
import functools
import math

import jax
import jax.numpy as jnp
from jax import lax
from jax.experimental import pallas as pl
from jax.experimental.pallas import tpu as pltpu
from jax.sharding import Mesh
from jax.sharding import PartitionSpec as P

EX_DEV = 64
HI=lax.Precision.HIGHEST
B=128; S=8
def lane_b(x,l): return jnp.broadcast_to(x[:,l:l+1],x.shape)
def sub_b(x,i): return jnp.broadcast_to(x[i:i+1,:],x.shape)
def dot(a,b,ca,cb):
    return lax.dot_general(a,b,(((ca,),(cb,)),((),())),precision=HI,preferred_element_type=jnp.float32)
def factor_block(a_ref, off, u_out, i_out):
    n=B//S
    rows=[a_ref[pl.ds(off+S*g,S),pl.ds(off,B)] for g in range(n)]
    lane=lax.broadcasted_iota(jnp.int32,(S,B),1); sub=lax.broadcasted_iota(jnp.int32,(S,B),0)
    inv=[(lane==sub+S*g).astype(jnp.float32) for g in range(n)]
    for s in range(n):
        cols=[[lane_b(rows[g],S*s+k) for k in range(S)] for g in range(s,n)]
        a=[[sub_b(cols[0][k],i) if i>=k else None for k in range(S)] for i in range(S)]
        low=[[None]*S for _ in range(S)]; d=[None]*S
        ru=[None]*S; ri=[None]*S
        for k in range(S):
            d[k]=lax.rsqrt(a[k][k])
            for i in range(k+1,S): low[i][k]=a[i][k]*d[k]
            for i in range(k+1,S):
                for j in range(k+1,i+1): a[i][j]=a[i][j]-low[i][k]*low[j][k]
            pu=sub_b(rows[s],k); pi=sub_b(inv[s],k)
            for m in range(k):
                pu=pu-low[k][m]*ru[m]; pi=pi-low[k][m]*ri[m]
            ru[k]=pu*d[k]; ri[k]=pi*d[k]
        for g in range(s+1,n):
            c=cols[g-s]; lc=[None]*S
            for k in range(S):
                v=c[k]
                for m in range(k): v=v-low[k][m]*lc[m]
                lc[k]=v*d[k]
            for k in range(S):
                rows[g]=rows[g]-lc[k]*ru[k]; inv[g]=inv[g]-lc[k]*ri[k]
        u=ru[0]; v=ri[0]
        for k in range(1,S):
            u=jnp.where(sub==k,ru[k],u); v=jnp.where(sub==k,ri[k],v)
        u_out[pl.ds(S*s,S),:]=u; i_out[pl.ds(S*s,S),:]=v
def factor_kernel(scale,shard_ref,g_ref,f_ref,band_ref,w_ref,a,u,linv,ublk,fs):
    n=g_ref.shape[0]; nb=n//B
    a[...]=g_ref[...]
    fs[...]=f_ref[...]
    def body(kb,_):
        off=pl.multiple_of(kb*B,B)
        factor_block(a,off,ublk,linv)
        r=lax.broadcasted_iota(jnp.int32,(B,B),0); c=lax.broadcasted_iota(jnp.int32,(B,B),1)
        u[pl.ds(off,B),pl.ds(off,B)]=jnp.where(c>=r,ublk[...],0.0)
        for kk in range(nb):
            @pl.when(kb==kk)
            def _():
                lo=kk*B; hi=lo+B
                li=linv[...]
                w=dot(fs[:,lo:hi],li,1,1)
                w_ref[:,lo:hi]=w*scale
                if hi<n:
                    p=dot(li,a[lo:hi,hi:],1,0)
                    u[lo:hi,hi:]=p
                    fs[:,hi:]=fs[:,hi:]-dot(w,p,1,0)
                    for ib in range(kk+1,nb):
                        q=(ib-kk-1)*B
                        a[ib*B:(ib+1)*B,ib*B:]=a[ib*B:(ib+1)*B,ib*B:]-dot(p[:,q:q+B],p[:,q:],0,0)
        return 0
    lax.fori_loop(0,nb,body,0)
    rows=band_ref.shape[0]
    start=pl.multiple_of(shard_ref[0]*rows,rows)
    x=u[pl.ds(start,rows),:]
    r=lax.broadcasted_iota(jnp.int32,x.shape,0)+start; c=lax.broadcasted_iota(jnp.int32,x.shape,1)
    band_ref[...]=jnp.where(c>=r,x,0.0)/scale

def factor_and_whiten(gram, features, shard, scale, side_rows):
    n = gram.shape[0]
    return pl.pallas_call(
        functools.partial(factor_kernel, scale),
        out_shape=(
            jax.ShapeDtypeStruct((side_rows, n), jnp.float32),
            jax.ShapeDtypeStruct(features.shape, jnp.float32),
        ),
        in_specs=[
            pl.BlockSpec(memory_space=pltpu.SMEM),
            pl.BlockSpec(memory_space=pltpu.VMEM),
            pl.BlockSpec(memory_space=pltpu.VMEM),
        ],
        out_specs=[pl.BlockSpec(memory_space=pltpu.VMEM)] * 2,
        scratch_shapes=[
            pltpu.VMEM((n, n), jnp.float32),
            pltpu.VMEM((n, n), jnp.float32),
            pltpu.VMEM((B, B), jnp.float32),
            pltpu.VMEM((B, B), jnp.float32),
            pltpu.VMEM(features.shape, jnp.float32),
        ],
        name="factor_whiten",
    )(shard, gram, features)


def shards(
    adapter_input,
    output_gradient,
    projection,
    input_block_index,
    turn_token_length,
    turn_to_example,
):
    adapter_rows = adapter_input[0]
    grad_rows = output_gradient[0]
    proj_blocks = projection[0]
    picked = input_block_index[0]
    adapter_rank = adapter_rows.shape[0]
    count_of_tokens = grad_rows.shape[0]
    key_value_width = grad_rows.shape[1]
    layers = lax.axis_size("layer")
    z_size = lax.axis_size("z")
    y_size = lax.axis_size("y")
    shard_count = z_size * y_size
    shard = lax.axis_index("z") * y_size + lax.axis_index("y")
    owners = turn_to_example - shard * EX_DEV
    turn_ends = jnp.cumsum(turn_token_length)
    starts = turn_ends - turn_token_length
    position = jnp.arange(count_of_tokens, dtype=jnp.int32)
    inside = (
        (position[None, :] >= starts[:, None]) & (position[None, :] < turn_ends[:, None])
    ).astype(jnp.bfloat16)
    member = (owners[None, :] == jnp.arange(EX_DEV, dtype=jnp.int32)[:, None]).astype(jnp.bfloat16)
    ownership_mask = jnp.dot(member, inside, preferred_element_type=jnp.float32).astype(
        jnp.bfloat16
    )
    weighted_rows = (ownership_mask[:, None, :] * adapter_rows[None, :, :]).reshape(
        EX_DEV * adapter_rank, count_of_tokens
    )
    summed_total = jnp.dot(weighted_rows, grad_rows, preferred_element_type=jnp.float32)
    gradient_value = summed_total.reshape(EX_DEV, adapter_rank * key_value_width).astype(
        jnp.bfloat16
    )
    pieces = []
    for column in range(proj_blocks.shape[0]):
        chosen = jnp.concatenate(
            [
                lax.dynamic_slice_in_dim(gradient_value, picked[column, slot_index] * 128, 128, 1)
                for slot_index in range(picked.shape[1])
            ],
            axis=1,
        )
        pieces.append(jnp.dot(chosen, proj_blocks[column], preferred_element_type=jnp.float32))
    partial = jnp.concatenate(pieces, axis=1)
    width = partial.shape[1]
    own_rows = EX_DEV // layers
    by_layer = lax.all_to_all(partial.reshape(layers, own_rows, width), "layer", 0, 0)
    features = jnp.sum(by_layer, axis=0)
    group = layers * y_size
    plane = lax.all_to_all(
        jnp.broadcast_to(features[None], (group, own_rows, width)), ("layer", "y"), 0, 0
    ).reshape(group * own_rows, width)
    mine = lax.axis_index("layer") * y_size + lax.axis_index("y")
    slab = width // group
    columns = lax.dynamic_slice_in_dim(plane, mine * slab, slab, 1)
    gram_part = jnp.dot(
        columns.T, plane, precision=lax.Precision.HIGHEST, preferred_element_type=jnp.float32
    )
    lanes = 128
    by_z = lax.all_to_all(gram_part.reshape(z_size, (slab // z_size) * width // lanes, lanes), "z", 0, 0)
    gram_row = jnp.sum(by_z, axis=0)
    gram_slab = lax.all_to_all(jnp.broadcast_to(gram_row[None], by_z.shape), "z", 0, 0)
    gram_slab = gram_slab.reshape(slab * width // lanes, lanes)
    gram_matrix = lax.all_to_all(
        jnp.broadcast_to(gram_slab[None], (group,) + gram_slab.shape), ("layer", "y"), 0, 0
    ).reshape(width, width)
    scale = math.sqrt(EX_DEV * shard_count)
    band, whitened = factor_and_whiten(
        gram_matrix, features, shard[None].astype(jnp.int32), scale, width // shard_count
    )
    return (band, whitened)


def solution(mesh):
    layer_count, shard_count = mesh.devices.shape
    y_size = 4
    fine = Mesh(
        mesh.devices.reshape(layer_count, shard_count // y_size, y_size), ("layer", "z", "y")
    )
    in_specs = (
        P("layer", None, ("z", "y")),
        P("layer", ("z", "y"), None),
        P("layer", None, None, None),
        P("layer", None, None),
        P(("z", "y")),
        P(("z", "y")),
    )
    out_specs = (P(("z", "y"), None), P(("z", "y", "layer"), None))
    return jax.shard_map(shards, mesh=fine, in_specs=in_specs, out_specs=out_specs, check_vma=False)
```

```python
import functools
import math

import jax
import jax.numpy as jnp
from jax import lax
from jax.experimental import pallas as pl
from jax.experimental.pallas import tpu as pltpu
from jax.sharding import Mesh
from jax.sharding import PartitionSpec as P

EX_DEV = 64
HI=lax.Precision.HIGHEST
B=128; S=8; SUB=64
def lane_b(x,l): return jnp.broadcast_to(x[:,l:l+1],x.shape)
def sub_b(x,i): return jnp.broadcast_to(x[i:i+1,:],x.shape)
def dot(a,b,ca,cb):
    return lax.dot_general(a,b,(((ca,),(cb,)),((),())),precision=HI,preferred_element_type=jnp.float32)
def split(x):
    h=x.astype(jnp.bfloat16); r=x-h.astype(jnp.float32)
    m=r.astype(jnp.bfloat16); l=(r-m.astype(jnp.float32)).astype(jnp.bfloat16)
    return h,m,l
def dot_tn(x,y):
    h,m,l=split(x); H,M,L=split(y)
    p=jnp.concatenate([h,h,m,h,m,l],axis=0); q=jnp.concatenate([H,M,H,L,M,H],axis=0)
    return lax.dot_general(p,q,(((0,),(0,)),((),())),preferred_element_type=jnp.float32)
def factor_block(a_ref, off, u_out, i_out, one):
    n=B//S; per=SUB//S
    rows=[a_ref[pl.ds(off+S*g,S),pl.ds(off,B)] for g in range(n)]
    lane=lax.broadcasted_iota(jnp.int32,(S,B),1); sub=lax.broadcasted_iota(jnp.int32,(S,B),0)
    inv=[(lane==sub+S*g).astype(jnp.float32) for g in range(n)]
    for sb in range(0,n,per):
        done_u=[]; done_i=[]
        for s in range(sb,sb+per):
            cols=[[lane_b(rows[g],S*s+k) for k in range(S)] for g in range(s,sb+per)]
            opq=[c*one for c in cols[0]]
            a=[[sub_b(opq[k],i) if i>=k else None for k in range(S)] for i in range(S)]
            low=[[None]*S for _ in range(S)]; d=[None]*S
            ru=[None]*S; ri=[None]*S
            for k in range(S):
                d[k]=lax.rsqrt(a[k][k])
                for i in range(k+1,S): low[i][k]=a[i][k]*d[k]
                for i in range(k+1,S):
                    for j in range(k+1,i+1): a[i][j]=a[i][j]-low[i][k]*low[j][k]
                pu=sub_b(rows[s],k); pi=sub_b(inv[s],k)
                for m in range(k):
                    pu=pu-low[k][m]*ru[m]; pi=pi-low[k][m]*ri[m]
                ru[k]=pu*d[k]; ri[k]=pi*d[k]
            for g in range(s+1,sb+per):
                c=cols[g-s]; lc=[None]*S
                for k in range(S):
                    v=c[k]
                    for m in range(k): v=v-low[k][m]*lc[m]
                    lc[k]=v*d[k]
                for k in range(S):
                    rows[g]=rows[g]-lc[k]*ru[k]; inv[g]=inv[g]-lc[k]*ri[k]
            u=ru[0]; v=ri[0]
            for k in range(1,S):
                u=jnp.where(sub==k,ru[k],u); v=jnp.where(sub==k,ri[k],v)
            u_out[pl.ds(S*s,S),:]=u; i_out[pl.ds(S*s,S),:]=v
            done_u.append(u); done_i.append(v)
        if sb+per<n:
            du=jnp.concatenate(done_u,axis=0); di=jnp.concatenate(done_i,axis=0)
            upd=dot_tn(du,jnp.concatenate([du,di],axis=1))
            for g in range(sb+per,n):
                rows[g]=rows[g]-upd[S*g:S*(g+1),:B]; inv[g]=inv[g]-upd[S*g:S*(g+1),B:]
def factor_kernel(scale,shard_ref,g_ref,f_ref,band_ref,w_ref,a,u,linv,ublk,fs):
    n=a.shape[0]; nb=n//B
    for (kb,q,grp),(owner,unit) in WHERE.items():
        a[kb*B+S*grp:kb*B+S*(grp+1),q*B:(q+1)*B]=g_ref[owner,unit]
    fs[...]=f_ref[...]
    def body(kb,_):
        off=pl.multiple_of(kb*B,B)
        factor_block(a,off,ublk,linv,jnp.where(shard_ref[0]>=0,1.0,0.0))
        r=lax.broadcasted_iota(jnp.int32,(B,B),0); c=lax.broadcasted_iota(jnp.int32,(B,B),1)
        u[pl.ds(off,B),pl.ds(off,B)]=jnp.where(c>=r,ublk[...],0.0)
        for kk in range(nb):
            @pl.when(kb==kk)
            def _():
                lo=kk*B; hi=lo+B
                li=linv[...]
                w=dot(fs[:,lo:hi],li,1,1)
                w_ref[:,lo:hi]=w*scale
                if hi<n:
                    p=dot(li,a[lo:hi,hi:],1,0)
                    u[lo:hi,hi:]=p
                    fs[:,hi:]=fs[:,hi:]-dot(w,p,1,0)
                    for ib in range(kk+1,nb):
                        q=(ib-kk-1)*B
                        a[ib*B:(ib+1)*B,ib*B:]=a[ib*B:(ib+1)*B,ib*B:]-dot(p[:,q:q+B],p[:,q:],0,0)
        return 0
    lax.fori_loop(0,nb,body,0)
    rows=band_ref.shape[0]
    start=pl.multiple_of(shard_ref[0]*rows,rows)
    x=u[pl.ds(start,rows),:]
    r=lax.broadcasted_iota(jnp.int32,x.shape,0)+start; c=lax.broadcasted_iota(jnp.int32,x.shape,1)
    band_ref[...]=jnp.where(c>=r,x,0.0)/scale

def factor_and_whiten(gram, features, shard, scale, side_rows):
    n = features.shape[1]
    return pl.pallas_call(
        functools.partial(factor_kernel, scale),
        out_shape=(
            jax.ShapeDtypeStruct((side_rows, n), jnp.float32),
            jax.ShapeDtypeStruct(features.shape, jnp.float32),
        ),
        in_specs=[
            pl.BlockSpec(memory_space=pltpu.SMEM),
            pl.BlockSpec(memory_space=pltpu.VMEM),
            pl.BlockSpec(memory_space=pltpu.VMEM),
        ],
        out_specs=[pl.BlockSpec(memory_space=pltpu.VMEM)] * 2,
        scratch_shapes=[
            pltpu.VMEM((n, n), jnp.float32),
            pltpu.VMEM((n, n), jnp.float32),
            pltpu.VMEM((B, B), jnp.float32),
            pltpu.VMEM((B, B), jnp.float32),
            pltpu.VMEM(features.shape, jnp.float32),
        ],
        name="factor_whiten",
    )(shard, gram, features)


TILE = 512


def project_kernel(
    index_ref, shard_ref, length_ref, example_ref, adapter_ref, proj_ref, grad_hbm, out_ref,
    grad, left, total, sems,
):
    ranks, slots = adapter_ref.shape
    tiles = slots // TILE

    def fetch(i):
        rows = pl.ds(pl.multiple_of(i * TILE, TILE), TILE)
        return pltpu.make_async_copy(grad_hbm.at[rows, :], grad.at[rows, :], sems.at[i])

    fetch(0).start()
    lengths = length_ref[...].astype(jnp.float32)
    used = jnp.sum(lengths)
    count = lax.div(used.astype(jnp.int32) + (TILE - 1), TILE)

    def begin(i, carry):
        fetch(i).start()
        return carry

    lax.fori_loop(1, count, begin, 0)
    owner = example_ref[...] - shard_ref[0] * EX_DEV
    turns = (EX_DEV, owner.shape[1])
    example = lax.broadcasted_iota(jnp.int32, turns, 0)
    owner = jnp.broadcast_to(owner, turns)
    lengths = jnp.broadcast_to(lengths, turns)
    start = jnp.sum(jnp.where(owner < example, lengths, 0.0), axis=1, keepdims=True)
    end = jnp.sum(jnp.where(owner <= example, lengths, 0.0), axis=1, keepdims=True)
    start = start.astype(jnp.int32)
    end = end.astype(jnp.int32)
    total[...] = jnp.zeros_like(total)

    def step(i, carry):
        first = pl.multiple_of(i * TILE, TILE)
        slot = lax.broadcasted_iota(jnp.int32, (EX_DEV, TILE), 1) + first
        owned = (slot >= start) & (slot < end)
        values = adapter_ref[:, pl.ds(first, TILE)].astype(jnp.float32)
        for r in range(ranks):
            row = jnp.broadcast_to(values[r : r + 1, :], (EX_DEV, TILE))
            left[r * EX_DEV : (r + 1) * EX_DEV, :] = jnp.where(owned, row, 0.0).astype(
                jnp.bfloat16
            )
        fetch(i).wait()
        total[...] += jnp.dot(
            left[...], grad[pl.ds(first, TILE), :], preferred_element_type=jnp.float32
        )
        return carry

    lax.fori_loop(0, count, step, 0)
    per_rank = total.shape[1] // B
    for j in range(proj_ref.shape[0]):
        chosen = []
        for k in range(index_ref.shape[1]):
            block = index_ref[j, k]
            r = lax.div(block, per_rank)
            q = lax.rem(block, per_rank)
            chosen.append(
                total[
                    pl.ds(pl.multiple_of(r * EX_DEV, EX_DEV), EX_DEV),
                    pl.ds(pl.multiple_of(q * B, B), B),
                ].astype(jnp.bfloat16)
            )
        out_ref[:, j * B : (j + 1) * B] = jnp.dot(
            jnp.concatenate(chosen, axis=1), proj_ref[j], preferred_element_type=jnp.float32
        )


def project(index, shard, lengths, examples, adapter, proj, grad):
    slots, width = grad.shape
    ranks = adapter.shape[0]
    smem = pl.BlockSpec(memory_space=pltpu.SMEM)
    vmem = pl.BlockSpec(memory_space=pltpu.VMEM)
    return pl.pallas_call(
        project_kernel,
        out_shape=jax.ShapeDtypeStruct((EX_DEV, proj.shape[0] * proj.shape[2]), jnp.float32),
        in_specs=[smem, smem, vmem, vmem, vmem, vmem, pl.BlockSpec(memory_space=pl.ANY)],
        out_specs=vmem,
        scratch_shapes=[
            pltpu.VMEM((slots, width), grad.dtype),
            pltpu.VMEM((ranks * EX_DEV, TILE), jnp.bfloat16),
            pltpu.VMEM((ranks * EX_DEV, width), jnp.float32),
            pltpu.SemaphoreType.DMA((slots // TILE,)),
        ],
        name="project",
    )(index, shard, lengths[None], examples[None], adapter, proj, grad)


def gram_plan():
    table, where = [], {}
    extra = {t: list(range(10, 16)) for t in range(4)}
    pairs = [(p, q) for p in range(4) for q in range(p + 1, 4)]
    for p, q in pairs:
        for h in range(4):
            side = 0 if h < 2 else 1
            unit = extra[(p, q)[side]].pop(0)
            for i in range(4):
                where[p, q, 4 * h + i] = (len(table), i)
            where[(p, q)[side], (p, q)[side], unit] = (len(table), 4)
            table.append((p, q, h, side, unit))
    for t in range(4):
        for h in range(2):
            for i in range(4):
                where[t, t, 4 * h + i] = (len(table), i)
            where[t, t, 8 + h] = (len(table), 4)
            table.append((t, t, h, 0, 8 + h))
    return table, where


PLAN, WHERE = gram_plan()


def spread_kernel(parts_ref, features_ref, send_ref):
    total = parts_ref[0]
    for i in range(1, parts_ref.shape[0]):
        total = total + parts_ref[i]
    features_ref[...] = total
    for d, (p, q, _, _, _) in enumerate(PLAN):
        send_ref[d, 0] = total[:, p * B : (p + 1) * B]
        send_ref[d, 1] = total[:, q * B : (q + 1) * B]


def spread(parts):
    _, rows, width = parts.shape
    return pl.pallas_call(
        spread_kernel,
        out_shape=(
            jax.ShapeDtypeStruct((rows, width), jnp.float32),
            jax.ShapeDtypeStruct((len(PLAN), 2, rows, B), jnp.float32),
        ),
        in_specs=[pl.BlockSpec(memory_space=pltpu.VMEM)],
        out_specs=[pl.BlockSpec(memory_space=pltpu.VMEM)] * 2,
        name="spread",
    )(parts)


def gram_kernel(role_ref, rows_ref, out_ref, cross, square):
    left = rows_ref[:, 0].reshape(-1, B)
    right = rows_ref[:, 1].reshape(-1, B)
    cross[...] = dot(left, right, 0, 0)
    side = jnp.where(role_ref[1] == 0, left, right)
    square[...] = dot(side, side, 0, 0)
    first = pl.multiple_of(role_ref[0] * 4 * S, 4 * S)
    unit = pl.multiple_of(role_ref[2] * S, S)
    for z in range(out_ref.shape[0]):
        for i in range(4):
            out_ref[z, i] = cross[pl.ds(first + S * i, S), :]
        out_ref[z, 4] = square[pl.ds(unit, S), :]


def gram_units(role, rows, copies):
    return pl.pallas_call(
        gram_kernel,
        out_shape=jax.ShapeDtypeStruct((copies, 5, S, B), jnp.float32),
        in_specs=[pl.BlockSpec(memory_space=pltpu.SMEM), pl.BlockSpec(memory_space=pltpu.VMEM)],
        out_specs=pl.BlockSpec(memory_space=pltpu.VMEM),
        scratch_shapes=[pltpu.VMEM((B, B), jnp.float32), pltpu.VMEM((B, B), jnp.float32)],
        name="gram_units",
    )(role, rows)


def shards(
    adapter_input,
    output_gradient,
    projection,
    input_block_index,
    turn_token_length,
    turn_to_example,
):
    adapter_rows = adapter_input[0]
    grad_rows = output_gradient[0]
    proj_blocks = projection[0]
    picked = input_block_index[0]
    layers = lax.axis_size("layer")
    far_size = lax.axis_size("zh")
    near_size = lax.axis_size("zl")
    y_size = lax.axis_size("y")
    shard_count = far_size * near_size * y_size
    shard = lax.axis_index(("zh", "zl", "y"))
    shard = shard.astype(jnp.int32)[None]
    partial = project(
        picked, shard, turn_token_length, turn_to_example, adapter_rows, proj_blocks, grad_rows
    )
    width = partial.shape[1]
    own_rows = EX_DEV // layers
    by_layer = lax.all_to_all(partial.reshape(layers, own_rows, width), "layer", 0, 0)
    features, outgoing = spread(by_layer)
    group = layers * y_size
    plane = lax.all_to_all(outgoing, ("layer", "y"), 0, 0)
    mine = lax.axis_index("layer") * y_size + lax.axis_index("y")
    role = lax.dynamic_index_in_dim(
        jnp.array([entry[2:] for entry in PLAN], jnp.int32), mine, 0, keepdims=False
    )
    packed = gram_units(role, plane, near_size)
    by_near = lax.all_to_all(packed, "zl", 0, 0)
    nearby = jnp.sum(by_near, axis=0)
    by_far = lax.all_to_all(jnp.broadcast_to(nearby[None], (far_size,) + nearby.shape), "zh", 0, 0)
    summed = jnp.sum(by_far, axis=0)
    gram_tiles = lax.all_to_all(
        jnp.broadcast_to(summed[None], (group,) + summed.shape), ("layer", "y"), 0, 0
    )
    scale = math.sqrt(EX_DEV * shard_count)
    band, whitened = factor_and_whiten(
        gram_tiles, features, shard, scale, width // shard_count
    )
    return (band, whitened)


def solution(mesh):
    layer_count, shard_count = mesh.devices.shape
    y_size = 4
    near_size = 4
    fine = Mesh(
        mesh.devices.reshape(
            layer_count, shard_count // (near_size * y_size), near_size, y_size
        ),
        ("layer", "zh", "zl", "y"),
    )
    part = ("zh", "zl", "y")
    in_specs = (
        P("layer", None, part),
        P("layer", part, None),
        P("layer", None, None, None),
        P("layer", None, None),
        P(part),
        P(part),
    )
    out_specs = (P(part, None), P(part + ("layer",), None))
    return jax.shard_map(shards, mesh=fine, in_specs=in_specs, out_specs=out_specs, check_vma=False)
```

```python
import functools
import math

import jax
import jax.numpy as jnp
from jax import lax
from jax.experimental import pallas as pl
from jax.experimental.pallas import tpu as pltpu
from jax.sharding import Mesh
from jax.sharding import PartitionSpec as P

EX_DEV = 64
HI=lax.Precision.HIGHEST
B=128; S=8; SUB=64
def lane_b(x,l): return jnp.broadcast_to(x[:,l:l+1],x.shape)
def sub_b(x,i): return jnp.broadcast_to(x[i:i+1,:],x.shape)
def dot(a,b,ca,cb):
    return lax.dot_general(a,b,(((ca,),(cb,)),((),())),precision=HI,preferred_element_type=jnp.float32)
def split(x):
    h=x.astype(jnp.bfloat16); r=x-h.astype(jnp.float32)
    m=r.astype(jnp.bfloat16); l=(r-m.astype(jnp.float32)).astype(jnp.bfloat16)
    return h,m,l
def dot_tn(x,y):
    h,m,l=split(x); H,M,L=split(y)
    p=jnp.concatenate([h,h,m,h,m,l],axis=0); q=jnp.concatenate([H,M,H,L,M,H],axis=0)
    return lax.dot_general(p,q,(((0,),(0,)),((),())),preferred_element_type=jnp.float32)
def factor_block(a_ref, off, u_out, i_out, one):
    n=B//S; per=SUB//S
    rows=[a_ref[pl.ds(off+S*g,S),pl.ds(off,B)] for g in range(n)]
    lane=lax.broadcasted_iota(jnp.int32,(S,B),1); sub=lax.broadcasted_iota(jnp.int32,(S,B),0)
    inv=[(lane==sub+S*g).astype(jnp.float32) for g in range(n)]
    for sb in range(0,n,per):
        done_u=[]; done_i=[]
        for s in range(sb,sb+per):
            cols=[[lane_b(rows[g],S*s+k) for k in range(S)] for g in range(s,sb+per)]
            opq=[c*one for c in cols[0]]
            a=[[sub_b(opq[k],i) if i>=k else None for k in range(S)] for i in range(S)]
            low=[[None]*S for _ in range(S)]; d=[None]*S
            ru=[None]*S; ri=[None]*S
            for k in range(S):
                d[k]=lax.rsqrt(a[k][k])
                for i in range(k+1,S): low[i][k]=a[i][k]*d[k]
                for i in range(k+1,S):
                    for j in range(k+1,i+1): a[i][j]=a[i][j]-low[i][k]*low[j][k]
                pu=sub_b(rows[s],k); pi=sub_b(inv[s],k)
                for m in range(k):
                    pu=pu-low[k][m]*ru[m]; pi=pi-low[k][m]*ri[m]
                ru[k]=pu*d[k]; ri[k]=pi*d[k]
            for g in range(s+1,sb+per):
                c=cols[g-s]; lc=[None]*S
                for k in range(S):
                    v=c[k]
                    for m in range(k): v=v-low[k][m]*lc[m]
                    lc[k]=v*d[k]
                for k in range(S):
                    rows[g]=rows[g]-lc[k]*ru[k]; inv[g]=inv[g]-lc[k]*ri[k]
            u=ru[0]; v=ri[0]
            for k in range(1,S):
                u=jnp.where(sub==k,ru[k],u); v=jnp.where(sub==k,ri[k],v)
            u_out[pl.ds(S*s,S),:]=u; i_out[pl.ds(S*s,S),:]=v
            done_u.append(u); done_i.append(v)
        if sb+per<n:
            du=jnp.concatenate(done_u,axis=0); di=jnp.concatenate(done_i,axis=0)
            upd=dot_tn(du,jnp.concatenate([du,di],axis=1))
            for g in range(sb+per,n):
                rows[g]=rows[g]-upd[S*g:S*(g+1),:B]; inv[g]=inv[g]-upd[S*g:S*(g+1),B:]
def factor_kernel(scale,shard_ref,g_ref,f_ref,band_ref,w_ref,a,u,linv,ublk,fs):
    n=a.shape[0]; nb=n//B
    for (kb,q,grp),(owner,unit) in WHERE.items():
        a[kb*B+S*grp:kb*B+S*(grp+1),q*B:(q+1)*B]=g_ref[owner,unit]
    fs[...]=f_ref[...]
    def body(kb,_):
        off=pl.multiple_of(kb*B,B)
        factor_block(a,off,ublk,linv,jnp.where(shard_ref[0]>=0,1.0,0.0))
        r=lax.broadcasted_iota(jnp.int32,(B,B),0); c=lax.broadcasted_iota(jnp.int32,(B,B),1)
        u[pl.ds(off,B),pl.ds(off,B)]=jnp.where(c>=r,ublk[...],0.0)
        for kk in range(nb):
            @pl.when(kb==kk)
            def _():
                lo=kk*B; hi=lo+B
                li=linv[...]
                w=dot(fs[:,lo:hi],li,1,1)
                w_ref[:,lo:hi]=w*scale
                if hi<n:
                    p=dot(li,a[lo:hi,hi:],1,0)
                    u[lo:hi,hi:]=p
                    fs[:,hi:]=fs[:,hi:]-dot(w,p,1,0)
                    for ib in range(kk+1,nb):
                        q=(ib-kk-1)*B
                        a[ib*B:(ib+1)*B,ib*B:]=a[ib*B:(ib+1)*B,ib*B:]-dot(p[:,q:q+B],p[:,q:],0,0)
        return 0
    lax.fori_loop(0,nb,body,0)
    rows=band_ref.shape[0]
    start=pl.multiple_of(shard_ref[0]*rows,rows)
    x=u[pl.ds(start,rows),:]
    r=lax.broadcasted_iota(jnp.int32,x.shape,0)+start; c=lax.broadcasted_iota(jnp.int32,x.shape,1)
    band_ref[...]=jnp.where(c>=r,x,0.0)/scale

def factor_and_whiten(gram, features, shard, scale, side_rows):
    n = features.shape[1]
    return pl.pallas_call(
        functools.partial(factor_kernel, scale),
        out_shape=(
            jax.ShapeDtypeStruct((side_rows, n), jnp.float32),
            jax.ShapeDtypeStruct(features.shape, jnp.float32),
        ),
        in_specs=[
            pl.BlockSpec(memory_space=pltpu.SMEM),
            pl.BlockSpec(memory_space=pltpu.VMEM),
            pl.BlockSpec(memory_space=pltpu.VMEM),
        ],
        out_specs=[pl.BlockSpec(memory_space=pltpu.VMEM)] * 2,
        scratch_shapes=[
            pltpu.VMEM((n, n), jnp.float32),
            pltpu.VMEM((n, n), jnp.float32),
            pltpu.VMEM((B, B), jnp.float32),
            pltpu.VMEM((B, B), jnp.float32),
            pltpu.VMEM(features.shape, jnp.float32),
        ],
        compiler_params=pltpu.CompilerParams(vmem_limit_bytes=12 << 20),
        name="factor_whiten",
    )(shard, gram, features)


TILE = 512


def project_kernel(
    index_hbm, length_hbm, example_hbm, adapter_hbm, proj_hbm, grad_hbm, out_ref,
    index_ref, length_ref, example_ref, adapter_ref, proj_ref, grad, left, total, sems, arrivals,
):
    ranks, slots = adapter_ref.shape

    def fetch(i):
        rows = pl.ds(pl.multiple_of(i * TILE, TILE), TILE)
        return pltpu.make_async_copy(grad_hbm.at[rows, :], grad.at[rows, :], sems.at[i])

    lengths_in = pltpu.make_async_copy(length_hbm, length_ref, arrivals.at[0])
    examples_in = pltpu.make_async_copy(example_hbm, example_ref, arrivals.at[1])
    adapter_in = pltpu.make_async_copy(adapter_hbm, adapter_ref, arrivals.at[2])
    index_in = pltpu.make_async_copy(index_hbm, index_ref, arrivals.at[3])
    proj_in = pltpu.make_async_copy(proj_hbm, proj_ref, arrivals.at[4])
    lengths_in.start()
    examples_in.start()
    fetch(0).start()
    adapter_in.start()
    index_in.start()
    lengths_in.wait()
    lengths = length_ref[...].astype(jnp.float32)
    used = jnp.sum(lengths)
    count = lax.div(used.astype(jnp.int32) + (TILE - 1), TILE)

    def begin(i, carry):
        fetch(i).start()
        return carry

    lax.fori_loop(1, count, begin, 0)
    proj_in.start()
    examples_in.wait()
    owner = example_ref[...] - example_ref[:, :1]
    turns = (EX_DEV, owner.shape[1])
    example = lax.broadcasted_iota(jnp.int32, turns, 0)
    owner = jnp.broadcast_to(owner, turns)
    lengths = jnp.broadcast_to(lengths, turns)
    start = jnp.sum(jnp.where(owner < example, lengths, 0.0), axis=1, keepdims=True)
    end = jnp.sum(jnp.where(owner <= example, lengths, 0.0), axis=1, keepdims=True)
    start = start.astype(jnp.int32)
    end = end.astype(jnp.int32)
    total[...] = jnp.zeros_like(total)
    adapter_in.wait()

    def step(i, carry):
        first = pl.multiple_of(i * TILE, TILE)
        slot = lax.broadcasted_iota(jnp.int32, (EX_DEV, TILE), 1) + first
        owned = (slot >= start) & (slot < end)
        values = adapter_ref[:, pl.ds(first, TILE)].astype(jnp.float32)
        for r in range(ranks):
            row = jnp.broadcast_to(values[r : r + 1, :], (EX_DEV, TILE))
            left[r * EX_DEV : (r + 1) * EX_DEV, :] = jnp.where(owned, row, 0.0).astype(
                jnp.bfloat16
            )
        fetch(i).wait()
        total[...] += jnp.dot(
            left[...], grad[pl.ds(first, TILE), :], preferred_element_type=jnp.float32
        )
        return carry

    lax.fori_loop(0, count, step, 0)
    index_in.wait()
    proj_in.wait()
    per_rank = total.shape[1] // B
    for j in range(proj_ref.shape[0]):
        chosen = []
        for k in range(index_ref.shape[1]):
            block = index_ref[j, k]
            r = lax.div(block, per_rank)
            q = lax.rem(block, per_rank)
            chosen.append(
                total[
                    pl.ds(pl.multiple_of(r * EX_DEV, EX_DEV), EX_DEV),
                    pl.ds(pl.multiple_of(q * B, B), B),
                ].astype(jnp.bfloat16)
            )
        out_ref[:, j * B : (j + 1) * B] = jnp.dot(
            jnp.concatenate(chosen, axis=1), proj_ref[j], preferred_element_type=jnp.float32
        )


def project(index, lengths, examples, adapter, proj, grad):
    slots, width = grad.shape
    ranks = adapter.shape[0]
    return pl.pallas_call(
        project_kernel,
        out_shape=jax.ShapeDtypeStruct((EX_DEV, proj.shape[0] * proj.shape[2]), jnp.float32),
        in_specs=[pl.BlockSpec(memory_space=pltpu.HBM)] * 6,
        out_specs=pl.BlockSpec(memory_space=pltpu.VMEM),
        scratch_shapes=[
            pltpu.SMEM(index.shape, index.dtype),
            pltpu.VMEM((1,) + lengths.shape, lengths.dtype),
            pltpu.VMEM((1,) + examples.shape, examples.dtype),
            pltpu.VMEM(adapter.shape, adapter.dtype),
            pltpu.VMEM(proj.shape, proj.dtype),
            pltpu.VMEM((slots, width), grad.dtype),
            pltpu.VMEM((ranks * EX_DEV, TILE), jnp.bfloat16),
            pltpu.VMEM((ranks * EX_DEV, width), jnp.float32),
            pltpu.SemaphoreType.DMA((slots // TILE,)),
            pltpu.SemaphoreType.DMA((5,)),
        ],
        compiler_params=pltpu.CompilerParams(vmem_limit_bytes=59 << 20),
        name="project",
    )(index, lengths[None], examples[None], adapter, proj, grad)


def gram_plan():
    table, where = [], {}
    extra = {t: list(range(10, 16)) for t in range(4)}
    pairs = [(p, q) for p in range(4) for q in range(p + 1, 4)]
    for p, q in pairs:
        for h in range(4):
            side = 0 if h < 2 else 1
            unit = extra[(p, q)[side]].pop(0)
            for i in range(4):
                where[p, q, 4 * h + i] = (len(table), i)
            where[(p, q)[side], (p, q)[side], unit] = (len(table), 4)
            table.append((p, q, h, side, unit))
    for t in range(4):
        for h in range(2):
            for i in range(4):
                where[t, t, 4 * h + i] = (len(table), i)
            where[t, t, 8 + h] = (len(table), 4)
            table.append((t, t, h, 0, 8 + h))
    return table, where


PLAN, WHERE = gram_plan()


def spread_kernel(parts_ref, features_ref, send_ref):
    total = parts_ref[0]
    for i in range(1, parts_ref.shape[0]):
        total = total + parts_ref[i]
    features_ref[...] = total
    for d, (p, q, _, _, _) in enumerate(PLAN):
        send_ref[d, 0] = total[:, p * B : (p + 1) * B]
        send_ref[d, 1] = total[:, q * B : (q + 1) * B]


def spread(parts):
    _, rows, width = parts.shape
    return pl.pallas_call(
        spread_kernel,
        out_shape=(
            jax.ShapeDtypeStruct((rows, width), jnp.float32),
            jax.ShapeDtypeStruct((len(PLAN), 2, rows, B), jnp.float32),
        ),
        in_specs=[pl.BlockSpec(memory_space=pltpu.VMEM)],
        out_specs=[pl.BlockSpec(memory_space=pltpu.VMEM)] * 2,
        compiler_params=pltpu.CompilerParams(vmem_limit_bytes=4 << 20),
        name="spread",
    )(parts)


def gram_kernel(mine_ref, table_ref, rows_ref, out_ref, cross, square):
    mine = mine_ref[0]
    left = rows_ref[:, 0].reshape(-1, B)
    right = rows_ref[:, 1].reshape(-1, B)
    cross[...] = dot(left, right, 0, 0)
    side = jnp.where(table_ref[mine, 1] == 0, left, right)
    square[...] = dot(side, side, 0, 0)
    first = pl.multiple_of(table_ref[mine, 0] * 4 * S, 4 * S)
    unit = pl.multiple_of(table_ref[mine, 2] * S, S)
    for z in range(out_ref.shape[0]):
        for i in range(4):
            out_ref[z, i] = cross[pl.ds(first + S * i, S), :]
        out_ref[z, 4] = square[pl.ds(unit, S), :]


def gram_units(mine, rows, copies):
    return pl.pallas_call(
        gram_kernel,
        out_shape=jax.ShapeDtypeStruct((copies, 5, S, B), jnp.float32),
        in_specs=[pl.BlockSpec(memory_space=pltpu.SMEM)] * 2 + [pl.BlockSpec(memory_space=pltpu.VMEM)],
        out_specs=pl.BlockSpec(memory_space=pltpu.VMEM),
        scratch_shapes=[pltpu.VMEM((B, B), jnp.float32), pltpu.VMEM((B, B), jnp.float32)],
        compiler_params=pltpu.CompilerParams(vmem_limit_bytes=4 << 20),
        name="gram_units",
    )(mine, jnp.array([entry[2:] for entry in PLAN], jnp.int32), rows)


def shards(
    adapter_input,
    output_gradient,
    projection,
    input_block_index,
    turn_token_length,
    turn_to_example,
):
    adapter_rows = adapter_input[0]
    grad_rows = output_gradient[0]
    proj_blocks = projection[0]
    picked = input_block_index[0]
    layers = lax.axis_size("layer")
    far_size = lax.axis_size("zh")
    near_size = lax.axis_size("zl")
    y_size = lax.axis_size("y")
    shard_count = far_size * near_size * y_size
    shard = lax.axis_index(("zh", "zl", "y"))
    shard = shard.astype(jnp.int32)[None]
    partial = project(
        picked, turn_token_length, turn_to_example, adapter_rows, proj_blocks, grad_rows
    )
    mine = (lax.axis_index("layer") * y_size + lax.axis_index("y")).astype(jnp.int32)[None]
    partial, mine, shard = lax.optimization_barrier((partial, mine, shard))
    width = partial.shape[1]
    own_rows = EX_DEV // layers
    by_layer = lax.all_to_all(partial.reshape(layers, own_rows, width), "layer", 0, 0)
    features, outgoing = spread(by_layer)
    group = layers * y_size
    plane = lax.all_to_all(outgoing, ("layer", "y"), 0, 0)
    packed = gram_units(mine, plane, near_size)
    by_near = lax.all_to_all(packed, "zl", 0, 0)
    nearby = jnp.sum(by_near, axis=0)
    by_far = lax.all_to_all(jnp.broadcast_to(nearby[None], (far_size,) + nearby.shape), "zh", 0, 0)
    summed = jnp.sum(by_far, axis=0)
    gram_tiles = lax.all_to_all(
        jnp.broadcast_to(summed[None], (group,) + summed.shape), ("layer", "y"), 0, 0
    )
    scale = math.sqrt(EX_DEV * shard_count)
    band, whitened = factor_and_whiten(
        gram_tiles, features, shard, scale, width // shard_count
    )
    return (band, whitened)


def solution(mesh):
    layer_count, shard_count = mesh.devices.shape
    y_size = 4
    near_size = 4
    fine = Mesh(
        mesh.devices.reshape(
            layer_count, shard_count // (near_size * y_size), near_size, y_size
        ),
        ("layer", "zh", "zl", "y"),
    )
    part = ("zh", "zl", "y")
    in_specs = (
        P("layer", None, part),
        P("layer", part, None),
        P("layer", None, None, None),
        P("layer", None, None),
        P(part),
        P(part),
    )
    out_specs = (P(part, None), P(part + ("layer",), None))
    return jax.shard_map(shards, mesh=fine, in_specs=in_specs, out_specs=out_specs, check_vma=False)
```

```python
import functools
import math

import jax
import jax.numpy as jnp
from jax import lax
from jax.experimental import pallas as pl
from jax.experimental.pallas import tpu as pltpu
from jax.sharding import Mesh
from jax.sharding import PartitionSpec as P

EX_DEV = 64
HI=lax.Precision.HIGHEST
B=128; S=8; SUB=64
def lane_b(x,l): return jnp.broadcast_to(x[:,l:l+1],x.shape)
def sub_b(x,i): return jnp.broadcast_to(x[i:i+1,:],x.shape)
def dot(a,b,ca,cb):
    return lax.dot_general(a,b,(((ca,),(cb,)),((),())),precision=HI,preferred_element_type=jnp.float32)
def dot3(a,b,ca,cb):
    h=a.astype(jnp.bfloat16); l=(a-h.astype(jnp.float32)).astype(jnp.bfloat16)
    H=b.astype(jnp.bfloat16); L=(b-H.astype(jnp.float32)).astype(jnp.bfloat16)
    f=lambda x,y: lax.dot_general(x,y,(((ca,),(cb,)),((),())),preferred_element_type=jnp.float32)
    return f(h,H)+(f(h,L)+f(l,H))
def split(x):
    h=x.astype(jnp.bfloat16); r=x-h.astype(jnp.float32)
    m=r.astype(jnp.bfloat16); l=(r-m.astype(jnp.float32)).astype(jnp.bfloat16)
    return h,m,l
def dot_tn(x,y):
    h,m,l=split(x); H,M,L=split(y)
    p=jnp.concatenate([h,h,m,h,m,l],axis=0); q=jnp.concatenate([H,M,H,L,M,H],axis=0)
    return lax.dot_general(p,q,(((0,),(0,)),((),())),preferred_element_type=jnp.float32)
def factor_block(a_ref, off, u_out, i_out, one):
    n=B//S; per=SUB//S
    rows=[a_ref[pl.ds(off+S*g,S),pl.ds(off,B)] for g in range(n)]
    lane=lax.broadcasted_iota(jnp.int32,(S,B),1); sub=lax.broadcasted_iota(jnp.int32,(S,B),0)
    inv=[(lane==sub+S*g).astype(jnp.float32) for g in range(n)]
    for sb in range(0,n,per):
        done_u=[]; done_i=[]
        for s in range(sb,sb+per):
            cols=[[lane_b(rows[g],S*s+k) for k in range(S)] for g in range(s,sb+per)]
            opq=[c*one for c in cols[0]]
            a=[[sub_b(opq[k],i) if i>=k else None for k in range(S)] for i in range(S)]
            low=[[None]*S for _ in range(S)]; d=[None]*S
            ru=[None]*S; ri=[None]*S
            for k in range(S):
                d[k]=lax.rsqrt(a[k][k])
                for i in range(k+1,S): low[i][k]=a[i][k]*d[k]
                for i in range(k+1,S):
                    for j in range(k+1,i+1): a[i][j]=a[i][j]-low[i][k]*low[j][k]
                pu=sub_b(rows[s],k); pi=sub_b(inv[s],k)
                for m in range(k):
                    pu=pu-low[k][m]*ru[m]; pi=pi-low[k][m]*ri[m]
                ru[k]=pu*d[k]; ri[k]=pi*d[k]
            for g in range(s+1,sb+per):
                c=cols[g-s]; lc=[None]*S
                for k in range(S):
                    v=c[k]
                    for m in range(k): v=v-low[k][m]*lc[m]
                    lc[k]=v*d[k]
                for k in range(S):
                    rows[g]=rows[g]-lc[k]*ru[k]; inv[g]=inv[g]-lc[k]*ri[k]
            u=ru[0]; v=ri[0]
            for k in range(1,S):
                u=jnp.where(sub==k,ru[k],u); v=jnp.where(sub==k,ri[k],v)
            u_out[pl.ds(S*s,S),:]=u; i_out[pl.ds(S*s,S),:]=v
            done_u.append(u); done_i.append(v)
        if sb+per<n:
            du=jnp.concatenate(done_u,axis=0); di=jnp.concatenate(done_i,axis=0)
            upd=dot_tn(du,jnp.concatenate([du,di],axis=1))
            for g in range(sb+per,n):
                rows[g]=rows[g]-upd[S*g:S*(g+1),:B]; inv[g]=inv[g]-upd[S*g:S*(g+1),B:]
def factor_kernel(scale,shard_ref,g_ref,f_ref,band_ref,w_ref,a,u,linv,ublk,fs):
    n=a.shape[0]; nb=n//B
    for (kb,q,grp),(owner,unit) in WHERE.items():
        a[kb*B+S*grp:kb*B+S*(grp+1),q*B:(q+1)*B]=g_ref[owner,unit]
    fs[...]=f_ref[...]
    def body(kb,_):
        off=pl.multiple_of(kb*B,B)
        factor_block(a,off,ublk,linv,jnp.where(shard_ref[0]>=0,1.0,0.0))
        r=lax.broadcasted_iota(jnp.int32,(B,B),0); c=lax.broadcasted_iota(jnp.int32,(B,B),1)
        u[pl.ds(off,B),pl.ds(off,B)]=jnp.where(c>=r,ublk[...],0.0)
        for kk in range(nb):
            @pl.when(kb==kk)
            def _():
                lo=kk*B; hi=lo+B
                li=linv[...]
                w=dot3(fs[:,lo:hi],li,1,1)
                w_ref[:,lo:hi]=w*scale
                if hi<n:
                    p=dot3(li,a[lo:hi,hi:],1,0)
                    u[lo:hi,hi:]=p
                    fs[:,hi:]=fs[:,hi:]-dot3(w,p,1,0)
                    for ib in range(kk+1,nb):
                        q=(ib-kk-1)*B
                        a[ib*B:(ib+1)*B,ib*B:]=a[ib*B:(ib+1)*B,ib*B:]-dot3(p[:,q:q+B],p[:,q:],0,0)
        return 0
    lax.fori_loop(0,nb,body,0)
    rows=band_ref.shape[0]
    start=pl.multiple_of(shard_ref[0]*rows,rows)
    x=u[pl.ds(start,rows),:]
    r=lax.broadcasted_iota(jnp.int32,x.shape,0)+start; c=lax.broadcasted_iota(jnp.int32,x.shape,1)
    band_ref[...]=jnp.where(c>=r,x,0.0)/scale

def factor_and_whiten(gram, features, shard, scale, side_rows):
    n = features.shape[1]
    return pl.pallas_call(
        functools.partial(factor_kernel, scale),
        out_shape=(
            jax.ShapeDtypeStruct((side_rows, n), jnp.float32),
            jax.ShapeDtypeStruct(features.shape, jnp.float32),
        ),
        in_specs=[
            pl.BlockSpec(memory_space=pltpu.SMEM),
            pl.BlockSpec(memory_space=pltpu.VMEM),
            pl.BlockSpec(memory_space=pltpu.VMEM),
        ],
        out_specs=[pl.BlockSpec(memory_space=pltpu.VMEM)] * 2,
        scratch_shapes=[
            pltpu.VMEM((n, n), jnp.float32),
            pltpu.VMEM((n, n), jnp.float32),
            pltpu.VMEM((B, B), jnp.float32),
            pltpu.VMEM((B, B), jnp.float32),
            pltpu.VMEM(features.shape, jnp.float32),
        ],
        compiler_params=pltpu.CompilerParams(vmem_limit_bytes=12 << 20),
        name="factor_whiten",
    )(shard, gram, features)


TILE = 512


def project_kernel(
    index_hbm, length_hbm, example_hbm, adapter_hbm, proj_hbm, grad_hbm, out_ref,
    index_ref, length_ref, example_ref, adapter_ref, proj_ref, grad, left, total, sems, arrivals,
):
    ranks, slots = adapter_ref.shape

    def fetch(i):
        rows = pl.ds(pl.multiple_of(i * TILE, TILE), TILE)
        return pltpu.make_async_copy(grad_hbm.at[rows, :], grad.at[rows, :], sems.at[i])

    lengths_in = pltpu.make_async_copy(length_hbm, length_ref, arrivals.at[0])
    examples_in = pltpu.make_async_copy(example_hbm, example_ref, arrivals.at[1])
    adapter_in = pltpu.make_async_copy(adapter_hbm, adapter_ref, arrivals.at[2])
    index_in = pltpu.make_async_copy(index_hbm, index_ref, arrivals.at[3])
    proj_in = pltpu.make_async_copy(proj_hbm, proj_ref, arrivals.at[4])
    lengths_in.start()
    examples_in.start()
    fetch(0).start()
    adapter_in.start()
    index_in.start()
    lengths_in.wait()
    lengths = length_ref[...].astype(jnp.float32)
    used = jnp.sum(lengths)
    count = lax.div(used.astype(jnp.int32) + (TILE - 1), TILE)

    def begin(i, carry):
        fetch(i).start()
        return carry

    lax.fori_loop(1, count, begin, 0)
    proj_in.start()
    examples_in.wait()
    owner = example_ref[...] - example_ref[:, :1]
    turns = (EX_DEV, owner.shape[1])
    example = lax.broadcasted_iota(jnp.int32, turns, 0)
    owner = jnp.broadcast_to(owner, turns)
    lengths = jnp.broadcast_to(lengths, turns)
    start = jnp.sum(jnp.where(owner < example, lengths, 0.0), axis=1, keepdims=True)
    end = jnp.sum(jnp.where(owner <= example, lengths, 0.0), axis=1, keepdims=True)
    start = start.astype(jnp.int32)
    end = end.astype(jnp.int32)
    total[...] = jnp.zeros_like(total)
    adapter_in.wait()

    def step(i, carry):
        first = pl.multiple_of(i * TILE, TILE)
        slot = lax.broadcasted_iota(jnp.int32, (EX_DEV, TILE), 1) + first
        owned = (slot >= start) & (slot < end)
        values = adapter_ref[:, pl.ds(first, TILE)].astype(jnp.float32)
        for r in range(ranks):
            row = jnp.broadcast_to(values[r : r + 1, :], (EX_DEV, TILE))
            left[r * EX_DEV : (r + 1) * EX_DEV, :] = jnp.where(owned, row, 0.0).astype(
                jnp.bfloat16
            )
        fetch(i).wait()
        total[...] += jnp.dot(
            left[...], grad[pl.ds(first, TILE), :], preferred_element_type=jnp.float32
        )
        return carry

    lax.fori_loop(0, count, step, 0)
    index_in.wait()
    proj_in.wait()
    per_rank = total.shape[1] // B
    for j in range(proj_ref.shape[0]):
        chosen = []
        for k in range(index_ref.shape[1]):
            block = index_ref[j, k]
            r = lax.div(block, per_rank)
            q = lax.rem(block, per_rank)
            chosen.append(
                total[
                    pl.ds(pl.multiple_of(r * EX_DEV, EX_DEV), EX_DEV),
                    pl.ds(pl.multiple_of(q * B, B), B),
                ].astype(jnp.bfloat16)
            )
        out_ref[:, j * B : (j + 1) * B] = jnp.dot(
            jnp.concatenate(chosen, axis=1), proj_ref[j], preferred_element_type=jnp.float32
        )


def project(index, lengths, examples, adapter, proj, grad):
    slots, width = grad.shape
    ranks = adapter.shape[0]
    return pl.pallas_call(
        project_kernel,
        out_shape=jax.ShapeDtypeStruct((EX_DEV, proj.shape[0] * proj.shape[2]), jnp.float32),
        in_specs=[pl.BlockSpec(memory_space=pltpu.HBM)] * 6,
        out_specs=pl.BlockSpec(memory_space=pltpu.VMEM),
        scratch_shapes=[
            pltpu.SMEM(index.shape, index.dtype),
            pltpu.VMEM((1,) + lengths.shape, lengths.dtype),
            pltpu.VMEM((1,) + examples.shape, examples.dtype),
            pltpu.VMEM(adapter.shape, adapter.dtype),
            pltpu.VMEM(proj.shape, proj.dtype),
            pltpu.VMEM((slots, width), grad.dtype),
            pltpu.VMEM((ranks * EX_DEV, TILE), jnp.bfloat16),
            pltpu.VMEM((ranks * EX_DEV, width), jnp.float32),
            pltpu.SemaphoreType.DMA((slots // TILE,)),
            pltpu.SemaphoreType.DMA((5,)),
        ],
        compiler_params=pltpu.CompilerParams(vmem_limit_bytes=59 << 20),
        name="project",
    )(index, lengths[None], examples[None], adapter, proj, grad)


def gram_plan():
    table, where = [], {}
    extra = {t: list(range(10, 16)) for t in range(4)}
    pairs = [(p, q) for p in range(4) for q in range(p + 1, 4)]
    for p, q in pairs:
        for h in range(4):
            side = 0 if h < 2 else 1
            unit = extra[(p, q)[side]].pop(0)
            for i in range(4):
                where[p, q, 4 * h + i] = (len(table), i)
            where[(p, q)[side], (p, q)[side], unit] = (len(table), 4)
            table.append((p, q, h, side, unit))
    for t in range(4):
        for h in range(2):
            for i in range(4):
                where[t, t, 4 * h + i] = (len(table), i)
            where[t, t, 8 + h] = (len(table), 4)
            table.append((t, t, h, 0, 8 + h))
    return table, where


PLAN, WHERE = gram_plan()


def spread_kernel(parts_ref, features_ref, send_ref):
    total = parts_ref[0]
    for i in range(1, parts_ref.shape[0]):
        total = total + parts_ref[i]
    features_ref[...] = total
    for d, (p, q, _, _, _) in enumerate(PLAN):
        send_ref[d, 0] = total[:, p * B : (p + 1) * B]
        send_ref[d, 1] = total[:, q * B : (q + 1) * B]


def spread(parts):
    _, rows, width = parts.shape
    return pl.pallas_call(
        spread_kernel,
        out_shape=(
            jax.ShapeDtypeStruct((rows, width), jnp.float32),
            jax.ShapeDtypeStruct((len(PLAN), 2, rows, B), jnp.float32),
        ),
        in_specs=[pl.BlockSpec(memory_space=pltpu.VMEM)],
        out_specs=[pl.BlockSpec(memory_space=pltpu.VMEM)] * 2,
        compiler_params=pltpu.CompilerParams(vmem_limit_bytes=4 << 20),
        name="spread",
    )(parts)


def gram_kernel(mine_ref, table_ref, rows_ref, out_ref, cross, square):
    mine = mine_ref[0]
    left = rows_ref[:, 0].reshape(-1, B)
    right = rows_ref[:, 1].reshape(-1, B)
    cross[...] = dot(left, right, 0, 0)
    side = jnp.where(table_ref[mine, 1] == 0, left, right)
    square[...] = dot(side, side, 0, 0)
    first = pl.multiple_of(table_ref[mine, 0] * 4 * S, 4 * S)
    unit = pl.multiple_of(table_ref[mine, 2] * S, S)
    for z in range(out_ref.shape[0]):
        for i in range(4):
            out_ref[z, i] = cross[pl.ds(first + S * i, S), :]
        out_ref[z, 4] = square[pl.ds(unit, S), :]


def gram_units(mine, rows, copies):
    return pl.pallas_call(
        gram_kernel,
        out_shape=jax.ShapeDtypeStruct((copies, 5, S, B), jnp.float32),
        in_specs=[pl.BlockSpec(memory_space=pltpu.SMEM)] * 2 + [pl.BlockSpec(memory_space=pltpu.VMEM)],
        out_specs=pl.BlockSpec(memory_space=pltpu.VMEM),
        scratch_shapes=[pltpu.VMEM((B, B), jnp.float32), pltpu.VMEM((B, B), jnp.float32)],
        compiler_params=pltpu.CompilerParams(vmem_limit_bytes=4 << 20),
        name="gram_units",
    )(mine, jnp.array([entry[2:] for entry in PLAN], jnp.int32), rows)


def shards(
    adapter_input,
    output_gradient,
    projection,
    input_block_index,
    turn_token_length,
    turn_to_example,
):
    adapter_rows = adapter_input[0]
    grad_rows = output_gradient[0]
    proj_blocks = projection[0]
    picked = input_block_index[0]
    layers = lax.axis_size("layer")
    far_size = lax.axis_size("zh")
    near_size = lax.axis_size("zl")
    y_size = lax.axis_size("y")
    shard_count = far_size * near_size * y_size
    shard = lax.axis_index(("zh", "zl", "y"))
    shard = shard.astype(jnp.int32)[None]
    partial = project(
        picked, turn_token_length, turn_to_example, adapter_rows, proj_blocks, grad_rows
    )
    mine = (lax.axis_index("layer") * y_size + lax.axis_index("y")).astype(jnp.int32)[None]
    partial, mine, shard = lax.optimization_barrier((partial, mine, shard))
    width = partial.shape[1]
    own_rows = EX_DEV // layers
    by_layer = lax.all_to_all(partial.reshape(layers, own_rows, width), "layer", 0, 0)
    features, outgoing = spread(by_layer)
    group = layers * y_size
    plane = lax.all_to_all(outgoing, ("layer", "y"), 0, 0)
    packed = gram_units(mine, plane, near_size)
    by_near = lax.all_to_all(packed, "zl", 0, 0)
    nearby = jnp.sum(by_near, axis=0)
    by_far = lax.all_to_all(jnp.broadcast_to(nearby[None], (far_size,) + nearby.shape), "zh", 0, 0)
    summed = jnp.sum(by_far, axis=0)
    gram_tiles = lax.all_to_all(
        jnp.broadcast_to(summed[None], (group,) + summed.shape), ("layer", "y"), 0, 0
    )
    scale = math.sqrt(EX_DEV * shard_count)
    band, whitened = factor_and_whiten(
        gram_tiles, features, shard, scale, width // shard_count
    )
    return (band, whitened)


def solution(mesh):
    layer_count, shard_count = mesh.devices.shape
    y_size = 4
    near_size = 4
    fine = Mesh(
        mesh.devices.reshape(
            layer_count, shard_count // (near_size * y_size), near_size, y_size
        ),
        ("layer", "zh", "zl", "y"),
    )
    part = ("zh", "zl", "y")
    in_specs = (
        P("layer", None, part),
        P("layer", part, None),
        P("layer", None, None, None),
        P("layer", None, None),
        P(part),
        P(part),
    )
    out_specs = (P(part, None), P(part + ("layer",), None))
    return jax.shard_map(shards, mesh=fine, in_specs=in_specs, out_specs=out_specs, check_vma=False)
```

```python
import functools
import math

import jax
import jax.numpy as jnp
from jax import lax
from jax.experimental import pallas as pl
from jax.experimental.pallas import tpu as pltpu
from jax.sharding import Mesh
from jax.sharding import PartitionSpec as P

EX_DEV = 64
HI=lax.Precision.HIGHEST
B=128; S=8; SUB=64
def lane_b(x,l): return jnp.broadcast_to(x[:,l:l+1],x.shape)
def sub_b(x,i): return jnp.broadcast_to(x[i:i+1,:],x.shape)
def dot(a,b,ca,cb):
    return lax.dot_general(a,b,(((ca,),(cb,)),((),())),precision=HI,preferred_element_type=jnp.float32)
def dot3(a,b,ca,cb):
    h=a.astype(jnp.bfloat16); l=(a-h.astype(jnp.float32)).astype(jnp.bfloat16)
    H=b.astype(jnp.bfloat16); L=(b-H.astype(jnp.float32)).astype(jnp.bfloat16)
    f=lambda x,y: lax.dot_general(x,y,(((ca,),(cb,)),((),())),preferred_element_type=jnp.float32)
    return f(h,H)+(f(h,L)+f(l,H))
def split(x):
    h=x.astype(jnp.bfloat16); r=x-h.astype(jnp.float32)
    m=r.astype(jnp.bfloat16); l=(r-m.astype(jnp.float32)).astype(jnp.bfloat16)
    return h,m,l
def dot_tn(x,y):
    h,m,l=split(x); H,M,L=split(y)
    p=jnp.concatenate([h,h,m],axis=0); q=jnp.concatenate([H,M,H],axis=0)
    return lax.dot_general(p,q,(((0,),(0,)),((),())),preferred_element_type=jnp.float32)
def factor_block(a_ref, off, u_out, i_out, one):
    n=B//S; per=SUB//S
    rows=[a_ref[pl.ds(off+S*g,S),pl.ds(off,B)] for g in range(n)]
    lane=lax.broadcasted_iota(jnp.int32,(S,B),1); sub=lax.broadcasted_iota(jnp.int32,(S,B),0)
    inv=[(lane==sub+S*g).astype(jnp.float32) for g in range(n)]
    for sb in range(0,n,per):
        done_u=[]; done_i=[]
        for s in range(sb,sb+per):
            cols=[[lane_b(rows[g],S*s+k) for k in range(S)] for g in range(s,sb+per)]
            opq=[c*one for c in cols[0]]
            a=[[sub_b(opq[k],i) if i>=k else None for k in range(S)] for i in range(S)]
            low=[[None]*S for _ in range(S)]; d=[None]*S
            ru=[None]*S; ri=[None]*S
            for k in range(S):
                d[k]=lax.rsqrt(a[k][k])
                for i in range(k+1,S): low[i][k]=a[i][k]*d[k]
                for i in range(k+1,S):
                    for j in range(k+1,i+1): a[i][j]=a[i][j]-low[i][k]*low[j][k]
                pu=sub_b(rows[s],k); pi=sub_b(inv[s],k)
                for m in range(k):
                    pu=pu-low[k][m]*ru[m]; pi=pi-low[k][m]*ri[m]
                ru[k]=pu*d[k]; ri[k]=pi*d[k]
            for g in range(s+1,sb+per):
                c=cols[g-s]; lc=[None]*S
                for k in range(S):
                    v=c[k]
                    for m in range(k): v=v-low[k][m]*lc[m]
                    lc[k]=v*d[k]
                for k in range(S):
                    rows[g]=rows[g]-lc[k]*ru[k]; inv[g]=inv[g]-lc[k]*ri[k]
            u=ru[0]; v=ri[0]
            for k in range(1,S):
                u=jnp.where(sub==k,ru[k],u); v=jnp.where(sub==k,ri[k],v)
            u_out[pl.ds(S*s,S),:]=u; i_out[pl.ds(S*s,S),:]=v
            done_u.append(u); done_i.append(v)
        if sb+per<n:
            du=jnp.concatenate(done_u,axis=0); di=jnp.concatenate(done_i,axis=0)
            upd=dot_tn(du,jnp.concatenate([du,di],axis=1))
            for g in range(sb+per,n):
                rows[g]=rows[g]-upd[S*g:S*(g+1),:B]; inv[g]=inv[g]-upd[S*g:S*(g+1),B:]
def factor_kernel(scale,shard_ref,g_ref,f_ref,band_ref,w_ref,a,u,linv,ublk,fs):
    n=a.shape[0]; nb=n//B
    for (kb,q,grp),(owner,unit) in WHERE.items():
        a[kb*B+S*grp:kb*B+S*(grp+1),q*B:(q+1)*B]=g_ref[owner,unit]
    fs[...]=f_ref[...]
    def body(kb,_):
        off=pl.multiple_of(kb*B,B)
        factor_block(a,off,ublk,linv,jnp.where(shard_ref[0]>=0,1.0,0.0))
        r=lax.broadcasted_iota(jnp.int32,(B,B),0); c=lax.broadcasted_iota(jnp.int32,(B,B),1)
        u[pl.ds(off,B),pl.ds(off,B)]=jnp.where(c>=r,ublk[...],0.0)
        for kk in range(nb):
            @pl.when(kb==kk)
            def _():
                lo=kk*B; hi=lo+B
                li=linv[...]
                w=dot3(fs[:,lo:hi],li,1,1)
                w_ref[:,lo:hi]=w*scale
                if hi<n:
                    p=dot3(li,a[lo:hi,hi:],1,0)
                    u[lo:hi,hi:]=p
                    fs[:,hi:]=fs[:,hi:]-dot3(w,p,1,0)
                    for ib in range(kk+1,nb):
                        q=(ib-kk-1)*B
                        a[ib*B:(ib+1)*B,ib*B:]=a[ib*B:(ib+1)*B,ib*B:]-dot3(p[:,q:q+B],p[:,q:],0,0)
        return 0
    lax.fori_loop(0,nb,body,0)
    rows=band_ref.shape[0]
    start=pl.multiple_of(shard_ref[0]*rows,rows)
    x=u[pl.ds(start,rows),:]
    r=lax.broadcasted_iota(jnp.int32,x.shape,0)+start; c=lax.broadcasted_iota(jnp.int32,x.shape,1)
    band_ref[...]=jnp.where(c>=r,x,0.0)/scale

def factor_and_whiten(gram, features, shard, scale, side_rows):
    n = features.shape[1]
    return pl.pallas_call(
        functools.partial(factor_kernel, scale),
        out_shape=(
            jax.ShapeDtypeStruct((side_rows, n), jnp.float32),
            jax.ShapeDtypeStruct(features.shape, jnp.float32),
        ),
        in_specs=[
            pl.BlockSpec(memory_space=pltpu.SMEM),
            pl.BlockSpec(memory_space=pltpu.VMEM),
            pl.BlockSpec(memory_space=pltpu.VMEM),
        ],
        out_specs=[pl.BlockSpec(memory_space=pltpu.VMEM)] * 2,
        scratch_shapes=[
            pltpu.VMEM((n, n), jnp.float32),
            pltpu.VMEM((n, n), jnp.float32),
            pltpu.VMEM((B, B), jnp.float32),
            pltpu.VMEM((B, B), jnp.float32),
            pltpu.VMEM(features.shape, jnp.float32),
        ],
        compiler_params=pltpu.CompilerParams(vmem_limit_bytes=12 << 20),
        name="factor_whiten",
    )(shard, gram, features)


TILE = 512


def project_kernel(
    index_hbm, length_hbm, example_hbm, adapter_hbm, proj_hbm, grad_hbm, out_ref,
    index_ref, length_ref, example_ref, adapter_ref, proj_ref, grad, left, total, sems, arrivals,
):
    ranks, slots = adapter_ref.shape

    def fetch(i):
        rows = pl.ds(pl.multiple_of(i * TILE, TILE), TILE)
        return pltpu.make_async_copy(grad_hbm.at[rows, :], grad.at[rows, :], sems.at[i])

    lengths_in = pltpu.make_async_copy(length_hbm, length_ref, arrivals.at[0])
    examples_in = pltpu.make_async_copy(example_hbm, example_ref, arrivals.at[1])
    adapter_in = pltpu.make_async_copy(adapter_hbm, adapter_ref, arrivals.at[2])
    index_in = pltpu.make_async_copy(index_hbm, index_ref, arrivals.at[3])
    proj_in = pltpu.make_async_copy(proj_hbm, proj_ref, arrivals.at[4])
    lengths_in.start()
    examples_in.start()
    fetch(0).start()
    adapter_in.start()
    index_in.start()
    lengths_in.wait()
    lengths = length_ref[...].astype(jnp.float32)
    used = jnp.sum(lengths)
    count = lax.div(used.astype(jnp.int32) + (TILE - 1), TILE)

    def begin(i, carry):
        fetch(i).start()
        return carry

    lax.fori_loop(1, count, begin, 0)
    proj_in.start()
    examples_in.wait()
    owner = example_ref[...] - example_ref[:, :1]
    turns = (EX_DEV, owner.shape[1])
    example = lax.broadcasted_iota(jnp.int32, turns, 0)
    owner = jnp.broadcast_to(owner, turns)
    lengths = jnp.broadcast_to(lengths, turns)
    start = jnp.sum(jnp.where(owner < example, lengths, 0.0), axis=1, keepdims=True)
    end = jnp.sum(jnp.where(owner <= example, lengths, 0.0), axis=1, keepdims=True)
    start = start.astype(jnp.int32)
    end = end.astype(jnp.int32)
    total[...] = jnp.zeros_like(total)
    adapter_in.wait()

    def step(i, carry):
        first = pl.multiple_of(i * TILE, TILE)
        slot = lax.broadcasted_iota(jnp.int32, (EX_DEV, TILE), 1) + first
        owned = (slot >= start) & (slot < end)
        values = adapter_ref[:, pl.ds(first, TILE)].astype(jnp.float32)
        for r in range(ranks):
            row = jnp.broadcast_to(values[r : r + 1, :], (EX_DEV, TILE))
            left[r * EX_DEV : (r + 1) * EX_DEV, :] = jnp.where(owned, row, 0.0).astype(
                jnp.bfloat16
            )
        fetch(i).wait()
        total[...] += jnp.dot(
            left[...], grad[pl.ds(first, TILE), :], preferred_element_type=jnp.float32
        )
        return carry

    lax.fori_loop(0, count, step, 0)
    index_in.wait()
    proj_in.wait()
    per_rank = total.shape[1] // B
    for j in range(proj_ref.shape[0]):
        chosen = []
        for k in range(index_ref.shape[1]):
            block = index_ref[j, k]
            r = lax.div(block, per_rank)
            q = lax.rem(block, per_rank)
            chosen.append(
                total[
                    pl.ds(pl.multiple_of(r * EX_DEV, EX_DEV), EX_DEV),
                    pl.ds(pl.multiple_of(q * B, B), B),
                ].astype(jnp.bfloat16)
            )
        out_ref[:, j * B : (j + 1) * B] = jnp.dot(
            jnp.concatenate(chosen, axis=1), proj_ref[j], preferred_element_type=jnp.float32
        )


def project(index, lengths, examples, adapter, proj, grad):
    slots, width = grad.shape
    ranks = adapter.shape[0]
    return pl.pallas_call(
        project_kernel,
        out_shape=jax.ShapeDtypeStruct((EX_DEV, proj.shape[0] * proj.shape[2]), jnp.float32),
        in_specs=[pl.BlockSpec(memory_space=pltpu.HBM)] * 6,
        out_specs=pl.BlockSpec(memory_space=pltpu.VMEM),
        scratch_shapes=[
            pltpu.SMEM(index.shape, index.dtype),
            pltpu.VMEM((1,) + lengths.shape, lengths.dtype),
            pltpu.VMEM((1,) + examples.shape, examples.dtype),
            pltpu.VMEM(adapter.shape, adapter.dtype),
            pltpu.VMEM(proj.shape, proj.dtype),
            pltpu.VMEM((slots, width), grad.dtype),
            pltpu.VMEM((ranks * EX_DEV, TILE), jnp.bfloat16),
            pltpu.VMEM((ranks * EX_DEV, width), jnp.float32),
            pltpu.SemaphoreType.DMA((slots // TILE,)),
            pltpu.SemaphoreType.DMA((5,)),
        ],
        compiler_params=pltpu.CompilerParams(vmem_limit_bytes=59 << 20),
        name="project",
    )(index, lengths[None], examples[None], adapter, proj, grad)


def gram_plan():
    table, where = [], {}
    extra = {t: list(range(10, 16)) for t in range(4)}
    pairs = [(p, q) for p in range(4) for q in range(p + 1, 4)]
    for p, q in pairs:
        for h in range(4):
            side = 0 if h < 2 else 1
            unit = extra[(p, q)[side]].pop(0)
            for i in range(4):
                where[p, q, 4 * h + i] = (len(table), i)
            where[(p, q)[side], (p, q)[side], unit] = (len(table), 4)
            table.append((p, q, h, side, unit))
    for t in range(4):
        for h in range(2):
            for i in range(4):
                where[t, t, 4 * h + i] = (len(table), i)
            where[t, t, 8 + h] = (len(table), 4)
            table.append((t, t, h, 0, 8 + h))
    return table, where


PLAN, WHERE = gram_plan()


def spread_kernel(parts_ref, features_ref, send_ref):
    total = parts_ref[0]
    for i in range(1, parts_ref.shape[0]):
        total = total + parts_ref[i]
    features_ref[...] = total
    for d, (p, q, _, _, _) in enumerate(PLAN):
        send_ref[d, 0] = total[:, p * B : (p + 1) * B]
        send_ref[d, 1] = total[:, q * B : (q + 1) * B]


def spread(parts):
    _, rows, width = parts.shape
    return pl.pallas_call(
        spread_kernel,
        out_shape=(
            jax.ShapeDtypeStruct((rows, width), jnp.float32),
            jax.ShapeDtypeStruct((len(PLAN), 2, rows, B), jnp.float32),
        ),
        in_specs=[pl.BlockSpec(memory_space=pltpu.VMEM)],
        out_specs=[pl.BlockSpec(memory_space=pltpu.VMEM)] * 2,
        compiler_params=pltpu.CompilerParams(vmem_limit_bytes=4 << 20),
        name="spread",
    )(parts)


def gram_kernel(mine_ref, table_ref, rows_ref, out_ref, cross, square):
    mine = mine_ref[0]
    left = rows_ref[:, 0].reshape(-1, B)
    right = rows_ref[:, 1].reshape(-1, B)
    cross[...] = dot(left, right, 0, 0)
    side = jnp.where(table_ref[mine, 1] == 0, left, right)
    square[...] = dot(side, side, 0, 0)
    first = pl.multiple_of(table_ref[mine, 0] * 4 * S, 4 * S)
    unit = pl.multiple_of(table_ref[mine, 2] * S, S)
    for z in range(out_ref.shape[0]):
        for i in range(4):
            out_ref[z, i] = cross[pl.ds(first + S * i, S), :]
        out_ref[z, 4] = square[pl.ds(unit, S), :]


def gram_units(mine, rows, copies):
    return pl.pallas_call(
        gram_kernel,
        out_shape=jax.ShapeDtypeStruct((copies, 5, S, B), jnp.float32),
        in_specs=[pl.BlockSpec(memory_space=pltpu.SMEM)] * 2 + [pl.BlockSpec(memory_space=pltpu.VMEM)],
        out_specs=pl.BlockSpec(memory_space=pltpu.VMEM),
        scratch_shapes=[pltpu.VMEM((B, B), jnp.float32), pltpu.VMEM((B, B), jnp.float32)],
        compiler_params=pltpu.CompilerParams(vmem_limit_bytes=4 << 20),
        name="gram_units",
    )(mine, jnp.array([entry[2:] for entry in PLAN], jnp.int32), rows)


def shards(
    adapter_input,
    output_gradient,
    projection,
    input_block_index,
    turn_token_length,
    turn_to_example,
):
    adapter_rows = adapter_input[0]
    grad_rows = output_gradient[0]
    proj_blocks = projection[0]
    picked = input_block_index[0]
    layers = lax.axis_size("layer")
    far_size = lax.axis_size("zh")
    near_size = lax.axis_size("zl")
    y_size = lax.axis_size("y")
    shard_count = far_size * near_size * y_size
    shard = lax.axis_index(("zh", "zl", "y"))
    shard = shard.astype(jnp.int32)[None]
    partial = project(
        picked, turn_token_length, turn_to_example, adapter_rows, proj_blocks, grad_rows
    )
    mine = (lax.axis_index("layer") * y_size + lax.axis_index("y")).astype(jnp.int32)[None]
    partial, mine, shard = lax.optimization_barrier((partial, mine, shard))
    width = partial.shape[1]
    own_rows = EX_DEV // layers
    by_layer = lax.all_to_all(partial.reshape(layers, own_rows, width), "layer", 0, 0)
    features, outgoing = spread(by_layer)
    group = layers * y_size
    plane = lax.all_to_all(outgoing, ("layer", "y"), 0, 0)
    packed = gram_units(mine, plane, near_size)
    by_near = lax.all_to_all(packed, "zl", 0, 0)
    nearby = jnp.sum(by_near, axis=0)
    by_far = lax.all_to_all(jnp.broadcast_to(nearby[None], (far_size,) + nearby.shape), "zh", 0, 0)
    summed = jnp.sum(by_far, axis=0)
    gram_tiles = lax.all_to_all(
        jnp.broadcast_to(summed[None], (group,) + summed.shape), ("layer", "y"), 0, 0
    )
    scale = math.sqrt(EX_DEV * shard_count)
    band, whitened = factor_and_whiten(
        gram_tiles, features, shard, scale, width // shard_count
    )
    return (band, whitened)


def solution(mesh):
    layer_count, shard_count = mesh.devices.shape
    y_size = 4
    near_size = 4
    fine = Mesh(
        mesh.devices.reshape(
            layer_count, shard_count // (near_size * y_size), near_size, y_size
        ),
        ("layer", "zh", "zl", "y"),
    )
    part = ("zh", "zl", "y")
    in_specs = (
        P("layer", None, part),
        P("layer", part, None),
        P("layer", None, None, None),
        P("layer", None, None),
        P(part),
        P(part),
    )
    out_specs = (P(part, None), P(part + ("layer",), None))
    return jax.shard_map(shards, mesh=fine, in_specs=in_specs, out_specs=out_specs, check_vma=False)
```
